32 devices in a mesh: groups: 2 (over x), frames: 16 (over z, y, core).
Axes of the slice: x: 2, y: 2, z: 4, core: 2. Of those that a mesh axis runs over, the one named last changes fastest.
Arguments:
- video: float32 [4, 16, 256, 256], P('groups', 'frames'), parts along dimension 0, may hold values from -9 to 9
- clip_start: int32 [4], P('groups'), parts along dimension 0, may hold values from 0 to 7
- gain_space: float32 [256], replicated, may hold values from 0.1 to 1.9
- qkv_space: float32 [256, 768], replicated, may hold values from -0.375 to 0.375
- out_space: float32 [256, 256], replicated, may hold values from -0.375 to 0.375
- gain_time: float32 [256], replicated, may hold values from 0.1 to 1.9
- qkv_time: float32 [256, 768], replicated, may hold values from -0.375 to 0.375
- out_time: float32 [256, 256], replicated, may hold values from -0.375 to 0.375
- code_sums: float32 [8192, 256], P(('groups', 'frames')), parts along dimension 0, may hold values from -12 to 12
- code_counts: float32 [8192], P(('groups', 'frames')), parts along dimension 0, may hold values from 1 to 10
Outputs:
- latents: float32 [4, 16, 256, 256], P('groups', None, 'frames'), parts along dimension 0
- new_sums: float32 [8192, 256], P(('groups', 'frames')), parts along dimension 0
- new_counts: float32 [8192], P(('groups', 'frames')), parts along dimension 0
- new_codebook: float32 [8192, 256], P(('groups', 'frames')), parts along dimension 0
The draws below stay inside these ranges and needn't reach their ends.
There are 2 independent parts, one for each index of `groups`. The reference program is written for one: setup_inputs(seed, part) draws one part's arguments, and reference() takes and returns one part's arrays. A program takes and returns all parts, laid end to end along the dimension named above; an argument that names none is the same for every part. Nothing has to cross between parts.
All inputs are finite; a program needn't handle non-finite values.
Results may differ from the reference program's by a relative error of at most 0.0003.
Values sent between devices are 32-bit elements; how exact they have to be, the bound alone decides.
A program may use at most 64 MiB of HBM per device.

```python
import math
import jax
import jax.numpy as jnp
from jax import lax

D = 256
HEADS = 4
HW = 256
K = 4096
CLIPS = 2
FRAMES = 16


def centre_count():
    return max(K // 16, 2)


def centre_rows(key):
    return jax.random.truncated_normal(jax.random.fold_in(key, 7001), -4.0, 4.0, (centre_count(), D), jnp.float32)


def draw_video(key, part):
    centres = centre_rows(key)
    shape_tok = (CLIPS, FRAMES, HW)
    first_pick = jax.random.randint(jax.random.fold_in(key, 7002), shape_tok, 0, centre_count())
    second_pick = jax.random.randint(jax.random.fold_in(key, 7003), shape_tok, 0, centre_count())
    chosen = jnp.minimum(first_pick, second_pick)
    picked = jnp.take(centres, chosen, axis=0)
    amplitude = 1.2
    noise = 0.9 * jax.random.truncated_normal(jax.random.fold_in(key, 7004), -4.0, 4.0, shape_tok + (D,), jnp.float32)
    return (amplitude * picked + noise).astype(jnp.float32)


def draw_code_sums(key, part):
    centres = centre_rows(key)
    owner = jax.random.permutation(jax.random.fold_in(key, 7006), jnp.arange(K, dtype=jnp.int32)) % centre_count()
    picked = jnp.take(centres, owner, axis=0)
    row_scale = jax.random.uniform(jax.random.fold_in(key, 7007), (K, 1), jnp.float32, 0.5, 1.5)
    noise = 0.8 * jax.random.truncated_normal(jax.random.fold_in(key, 7008), -4.0, 4.0, (K, D), jnp.float32)
    return (row_scale * (picked + noise)).astype(jnp.float32)


def block_scale(key, shape, pieces, low, top_value):
    def one(dim, parts):
        draws = jax.random.uniform(jax.random.fold_in(jax.random.fold_in(key, 6), dim), (parts,), jnp.float32, low / len(pieces), top_value / len(pieces))
        return jnp.repeat(jnp.exp(draws), shape[dim] // parts).reshape((-1,) + (1,) * (len(shape) - dim - 1))

    loudness = one(*pieces[0])
    for cut in pieces[1:]:
        loudness = loudness * one(*cut)
    return loudness


def normal_values(rng, shape, scale, reach, held_as=jnp.bfloat16):
    drawn = jax.random.normal(rng, shape, jnp.float32) * scale
    return jnp.minimum(jnp.maximum(drawn, -reach), reach).astype(held_as)


def setup_inputs(seed: int = 0, part: int = 0) -> dict:
    keys = jax.random.split(jax.random.key(seed), 11)
    part_keys = jax.random.split(jax.random.fold_in(keys[10], part), 11)
    return {
        "video": draw_video(jax.random.fold_in(jax.random.fold_in(keys[10], part), 71), part),
        "clip_start": jax.random.randint(part_keys[1], (CLIPS,), 0, FRAMES // 2).astype(jnp.int32),
        "gain_space": jnp.clip(1.0 + 0.18 * jax.random.normal(keys[2], (D,), jnp.float32), 0.1, 1.9),
        "qkv_space": normal_values(keys[3], (D, 3 * D), D ** -0.5, 0.375, jnp.float32),
        "out_space": normal_values(keys[4], (D, D), D ** -0.5, 0.375, jnp.float32),
        "gain_time": jnp.clip(1.0 + 0.18 * jax.random.normal(keys[5], (D,), jnp.float32), 0.1, 1.9),
        "qkv_time": normal_values(keys[6], (D, 3 * D), D ** -0.5, 0.375, jnp.float32),
        "out_time": normal_values(keys[7], (D, D), D ** -0.5, 0.375, jnp.float32),
        "code_sums": draw_code_sums(jax.random.fold_in(jax.random.fold_in(keys[10], part), 71), part),
        "code_counts": jnp.clip(jnp.exp(math.log(10.0) - 2.3025851 * jax.random.uniform(part_keys[9], (K,), jnp.float32) ** block_scale(part_keys[9], (K,), ((0, 16),), -0.2, 0.2)), 1.0, 10.0),
    }


ATTN_SCALE = 10.0
SOFTMAX_WARMTH = 0.05
DECAY_RATE = 0.9
EPSILON = 1e-06
TOP_PRECISION = lax.Precision.HIGHEST

def rms_norm(values, gain_vec):
    return values * lax.rsqrt(lax.optimization_barrier(jnp.mean(values * values, -1, keepdims=True)) + EPSILON) * gain_vec

def unit_vec(values):
    return values * lax.rsqrt(lax.optimization_barrier(jnp.sum(values * values, -1, keepdims=True)) + EPSILON)

def spatial_block(one_frame, gain_vec, w_qkv, w_out):
    width = one_frame.shape[-1]
    normed = rms_norm(one_frame, gain_vec)
    packed = jnp.dot(normed, w_qkv, precision=TOP_PRECISION)
    queries = unit_vec(packed[:, :width].reshape(-1, HEADS, width // HEADS))
    key_vecs = unit_vec(packed[:, width:2 * width].reshape(-1, HEADS, width // HEADS))
    values = packed[:, 2 * width:].reshape(-1, HEADS, width // HEADS)
    scores = ATTN_SCALE * jnp.einsum('qhd,khd->hqk', queries, key_vecs, precision=TOP_PRECISION)
    assignment_weights = jnp.exp(scores)
    totals = lax.optimization_barrier(jnp.sum(assignment_weights, -1)).T[:, :, None]
    mixed = jnp.einsum('hqk,khd->qhd', assignment_weights, values, precision=TOP_PRECISION) / totals
    return one_frame + jnp.dot(mixed.reshape(-1, width), w_out, precision=TOP_PRECISION)

def time_block(spaced, clip_start, gain_vec, w_qkv, w_out):
    clips, frames, places, width = spaced.shape
    normed = rms_norm(spaced, gain_vec)
    packed = jnp.einsum('ctpd,de->ctpe', normed, w_qkv, precision=TOP_PRECISION)
    shape_heads = (clips, frames, places, HEADS, width // HEADS)
    queries = unit_vec(packed[..., :width].reshape(shape_heads))
    key_vecs = unit_vec(packed[..., width:2 * width].reshape(shape_heads))
    values = packed[..., 2 * width:].reshape(shape_heads)
    scores = ATTN_SCALE * jnp.einsum('ctphd,csphd->cphts', queries, key_vecs, precision=TOP_PRECISION)
    later = jnp.arange(frames, dtype=jnp.int32)[:, None]
    earlier = jnp.arange(frames, dtype=jnp.int32)[None, :]
    allowed = (earlier <= later)[None] & ((earlier[None] >= clip_start[:, None, None]) | (earlier == later)[None])
    assignment_weights = jnp.exp(scores) * allowed[:, None, None, :, :].astype(jnp.float32)
    totals = jnp.transpose(lax.optimization_barrier(jnp.sum(assignment_weights, -1)), (0, 3, 1, 2))[..., None]
    mixed = jnp.einsum('cphts,csphd->ctphd', assignment_weights, values, precision=TOP_PRECISION) / totals
    return spaced + jnp.einsum('ctpd,de->ctpe', mixed.reshape(clips, frames, places, width), w_out, precision=TOP_PRECISION)

def reference(video, clip_start, gain_space, qkv_space, out_space, gain_time, qkv_time, out_time, code_sums, code_counts):
    clips, frames, places, width = video.shape
    flat_frames = video.reshape(clips * frames, places, width)
    spaced = lax.map(lambda one_frame: spatial_block(one_frame, gain_space, qkv_space, out_space), flat_frames)
    spaced = spaced.reshape(clips, frames, places, width)
    latents = time_block(spaced, clip_start, gain_time, qkv_time, out_time)
    unit_token_vectors = unit_vec(latents.reshape(clips * frames, places, width))
    unit_code_vectors = unit_vec(code_sums / code_counts[:, None])

    def accumulate(carry, rows_per_block):
        sums_acc, counts_acc = carry
        assignment_weights = jnp.exp(jnp.dot(rows_per_block, unit_code_vectors.T, precision=TOP_PRECISION) / SOFTMAX_WARMTH)
        probs = assignment_weights / lax.optimization_barrier(jnp.sum(assignment_weights, 1, keepdims=True))
        sums_acc = sums_acc + lax.dot_general(probs, rows_per_block, (((0,), (0,)), ((), ())), precision=TOP_PRECISION)
        counts_acc = counts_acc + lax.optimization_barrier(jnp.sum(probs, 0))
        return ((sums_acc, counts_acc), None)
    start_carry = (jnp.zeros(code_sums.shape, jnp.float32), jnp.zeros(code_counts.shape, jnp.float32))
    (term_sums, term_counts), _ = lax.scan(accumulate, start_carry, unit_token_vectors)
    new_sums = DECAY_RATE * code_sums + (1.0 - DECAY_RATE) * term_sums
    new_counts = DECAY_RATE * code_counts + (1.0 - DECAY_RATE) * term_counts
    new_codebook = new_sums / new_counts[:, None]
    return (latents, new_sums, new_counts, new_codebook)
```

```python
import functools

import jax
import jax.numpy as jnp
from jax import lax
from jax.experimental import pallas as pl
from jax.experimental.pallas import tpu as pltpu
from jax.sharding import PartitionSpec as P

HEADS = 4
ATTN_SCALE = 10.0
SOFTMAX_WARMTH = 0.05
DECAY_RATE = 0.9
EPSILON = 1e-06
F32 = jnp.float32
BF16 = jnp.bfloat16
NN = (((1,), (0,)), ((), ()))
NT = (((1,), (1,)), ((), ()))


def split(a):
    hi = a.astype(BF16)
    return hi, (a - hi.astype(F32)).astype(BF16)


def dot(a, b, dims=NN):
    return lax.dot_general(a, b, dims, preferred_element_type=F32)


def dot3(a, b, dims=NN):
    return dot(a[0], b[0], dims) + (dot(a[0], b[1], dims) + dot(a[1], b[0], dims))


def dot2(a, b, dims=NN):
    return dot(a[0], b, dims) + dot(a[1], b, dims)


def attention(x, gain, w_qkv, w_out, mask):
    rows, width = x.shape
    hd = width // HEADS
    lane_i = lax.broadcasted_iota(jnp.int32, (width, width), 0) // hd
    lane_j = lax.broadcasted_iota(jnp.int32, (width, width), 1) // hd
    same_head = jnp.where(lane_i == lane_j, 1.0, 0.0).astype(BF16)
    row_head = lax.broadcasted_iota(jnp.int32, (rows, width), 1) // hd

    normed = x * lax.rsqrt(jnp.mean(x * x, -1, keepdims=True) + EPSILON) * gain
    packed = dot3(split(normed), w_qkv)
    q, k, v = packed[:, :width], packed[:, width : 2 * width], packed[:, 2 * width :]
    q = q * lax.rsqrt(dot2(split(q * q), same_head) + EPSILON) * ATTN_SCALE
    k = k * lax.rsqrt(dot2(split(k * k), same_head) + EPSILON)
    qh, ql = split(q)
    ks = split(k)
    vh, vl = split(v)
    mixed = None
    for h in range(HEADS):
        mine = jnp.where(row_head == h, 1.0, 0.0).astype(BF16)
        e = jnp.exp(dot3((qh * mine, ql * mine), ks, NT))
        if mask is not None:
            e = e * mask
        es = split(e)
        o = dot3(es, (vh * mine, vl * mine))
        t = dot2(es, mine)
        mixed, totals = (o, t) if h == 0 else (mixed + o, totals + t)
    return x + dot3(split(mixed / totals), w_out)


def body(
    n,
    video,
    starts,
    gain_space,
    qkv_space,
    out_space,
    gain_time,
    qkv_time,
    out_time,
    code_sums,
    code_counts,
    latents,
    new_sums,
    new_counts,
    new_codebook,
    spaced,
    xin,
    codes,
    weights,
    u_hi,
    u_lo,
    cs,
    ck,
    cr,
    ys,
    yr,
    zs,
    zr,
    a2a_send,
    a2a_recv,
    gz_send,
    gz_recv,
    gy_send,
    gy_recv,
    gc_send,
    gc_recv,
    rc_send,
    rc_recv,
    ry_send,
    ry_recv,
    rz_send,
    rz_recv,
):
    clips, places, width = video.shape
    share = places // n
    rows = code_sums.shape[0]
    n4 = n // 4
    halves = ck.shape[1]
    part = rows // halves
    tokens = clips * places

    me = lax.axis_index("frames")
    zz, b1, b0 = me // 4, (me // 2) % 2, me % 2
    y_mate = zz * 4 + (1 - b1) * 2 + b0
    c_mate = zz * 4 + b1 * 2 + (1 - b0)
    pending = []

    def remote(src, dst, ssem, rsem, dev):
        return pltpu.make_async_remote_copy(
            src_ref=src, dst_ref=dst, send_sem=ssem, recv_sem=rsem,
            device_id={"frames": dev}, device_id_type=pl.DeviceIdType.MESH,
        )

    def send(src, dst, ssem, rsem, dev):
        cp = remote(src, dst, ssem, rsem, dev)
        cp.start()
        pending.append(cp)

    barrier = pltpu.get_barrier_semaphore()

    def greet(i, c):
        pl.semaphore_signal(
            barrier, inc=1, device_id={"frames": lax.rem(me + i, n)},
            device_id_type=pl.DeviceIdType.MESH,
        )
        return c

    lax.fori_loop(1, n, greet, 0)

    own = code_sums[...] / jnp.transpose(jnp.broadcast_to(code_counts[...], (width, rows)))
    own = own * lax.rsqrt(jnp.sum(own * own, -1, keepdims=True) + EPSILON)
    codes[me] = own
    pl.semaphore_wait(barrier, n - 1)

    def block(d, y, c):
        return lax.rem(zz + d, n4) * 4 + y * 2 + c

    def back(d, y, c):
        return lax.rem(zz + n4 - d, n4) * 4 + y * 2 + c

    def gather_z(d):
        send(codes.at[me], codes.at[me], gz_send.at[d], gz_recv.at[d], block(d, b1, b0))

    def forward_own(d):
        g = back(d, b1, b0)
        if d:
            remote(codes.at[g], codes.at[g], gz_send.at[d], gz_recv.at[d], me).wait_recv()
        send(codes.at[g], codes.at[g], gy_send.at[d], gy_recv.at[d], y_mate)
        send(codes.at[g], codes.at[g], gc_send.at[d], gc_recv.at[d], c_mate)

    def forward_y(d):
        g = back(d, 1 - b1, b0)
        remote(codes.at[g], codes.at[g], gy_send.at[d], gy_recv.at[d], me).wait_recv()
        send(codes.at[g], codes.at[g], gc_send.at[n4 + d], gc_recv.at[n4 + d], c_mate)

    def arrived(d):
        for g, s in ((back(d, b1, 1 - b0), d), (back(d, 1 - b1, 1 - b0), n4 + d)):
            remote(codes.at[g], codes.at[g], gc_send.at[s], gc_recv.at[s], me).wait_recv()

    forward_own(0)
    if n4 > 1:
        gather_z(1)

    w_q, w_o = split(qkv_space[...]), split(out_space[...])
    gain = gain_space[...]
    for c in range(clips):
        spaced[c] = attention(video[c], gain, w_q, w_o, None)
        for d in range(1, n):
            to = lax.rem(me + d, n)
            send(
                spaced.at[c, pl.ds(pl.multiple_of(to * share, 8), share), :],
                xin.at[c, me], a2a_send.at[c, d], a2a_recv.at[c, d], to,
            )
        xin[c, me] = spaced[c, pl.ds(pl.multiple_of(me * share, 8), share), :]
    for d in range(2, n4):
        gather_z(d)

    w_q, w_o = split(qkv_time[...]), split(out_time[...])
    gain = gain_time[...]
    bits = share.bit_length() - 1
    r_i = lax.broadcasted_iota(jnp.int32, (places, places), 0)
    r_j = lax.broadcasted_iota(jnp.int32, (places, places), 1)
    t_i, t_j = r_i >> bits, r_j >> bits
    same_place = (r_i & (share - 1)) == (r_j & (share - 1))
    nxt = 1
    forwarded_y = 0
    for c in range(clips):
        if nxt < n4:
            forward_own(nxt)
            nxt += 1
            forward_y(forwarded_y)
            forwarded_y += 1
        for d in range(1, n):
            src = lax.rem(me + n - d, n)
            remote(xin.at[c, src], xin.at[c, src], a2a_send.at[c, d], a2a_recv.at[c, d], me).wait_recv()
        allowed = same_place & (t_j <= t_i) & ((t_j >= starts[c]) | (t_j == t_i))
        mask = jnp.where(allowed, 1.0, 0.0)
        y = attention(xin[c].reshape(places, width), gain, w_q, w_o, mask)
        latents[c] = y.reshape(n, share, width)
        u = y * lax.rsqrt(jnp.sum(y * y, -1, keepdims=True) + EPSILON)
        u_hi[0, pl.ds(c * places, places), :], u_lo[0, pl.ds(c * places, places), :] = split(u)
        u = u * (1.0 / SOFTMAX_WARMTH)
        u_hi[1, pl.ds(c * places, places), :], u_lo[1, pl.ds(c * places, places), :] = split(u)
    while nxt < n4:
        forward_own(nxt)
        nxt += 1
        forward_y(forwarded_y)
        forwarded_y += 1

    def score(g, acc):
        e = jnp.exp(dot3(split(codes[g]), (u_hi[1], u_lo[1]), NT))
        weights[g] = e
        return acc + jnp.sum(e.reshape(rows // 8, 8, tokens), 0)

    acc = jnp.zeros((8, tokens), F32)
    for d in range(n4):
        if forwarded_y <= d:
            forward_y(forwarded_y)
            forwarded_y += 1
        arrived(d)
        base = lax.rem(zz + n4 - d, n4) * 4
        acc = lax.fori_loop(0, 4, lambda i, a: score(base + i, a), acc)
    inv = 1.0 / jnp.sum(acc, 0, keepdims=True)
    ones = jnp.ones((8, tokens), BF16)

    def term(g, h, dst):
        ps = split(weights[g, pl.ds(h * part, part), :] * inv)
        dst[pl.ds(0, part), :] = dot3(ps, (u_hi[0], u_lo[0]))
        cnt = dot(ones, ps[0], NT) + dot(ones, ps[1], NT)
        if part < width:
            cnt = jnp.concatenate([cnt, jnp.zeros((8, width - part), F32)], 1)
        dst[pl.ds(part, 8), :] = cnt

    def start(d, h):
        for j in range(2):
            y = lax.rem(b1 + 1 + j, 2)
            term(block(d, y, 1 - b0), h, cs.at[d, h, j])
            send(cs.at[d, h, j], cr.at[d, h, j], rc_send.at[d, h, j], rc_recv.at[d, h, j], c_mate)
        for j in range(2):
            y = lax.rem(b1 + 1 + j, 2)
            term(block(d, y, b0), h, ck.at[d, h, j])

    def wait_core(d, h, j):
        remote(cr.at[d, h, j], cr.at[d, h, j], rc_send.at[d, h, j], rc_recv.at[d, h, j], me).wait_recv()

    def pair(d, h):
        wait_core(d, h, 0)
        ys[d, h] = ck[d, h, 0] + cr[d, h, 0]
        send(ys.at[d, h], yr.at[d, h], ry_send.at[d, h], ry_recv.at[d, h], y_mate)

    def across(d, h):
        wait_core(d, h, 1)
        remote(yr.at[d, h], yr.at[d, h], ry_send.at[d, h], ry_recv.at[d, h], me).wait_recv()
        zs[d, h] = ck[d, h, 1] + cr[d, h, 1] + yr[d, h]
        if d:
            send(zs.at[d, h], zr.at[d, h], rz_send.at[d, h], rz_recv.at[d, h], block(d, b1, b0))

    steps = [(d % n4, h) for d in range(1, n4 + 1) for h in range(halves)]
    total = len(steps)
    for i in range(total + 2):
        if i < total:
            start(*steps[i])
        if 1 <= i <= total:
            pair(*steps[i - 1])
        if i >= 2:
            across(*steps[i - 2])

    for h in range(halves):
        tot = zs[0, h]
        for d in range(1, n4):
            remote(zr.at[d, h], zr.at[d, h], rz_send.at[d, h], rz_recv.at[d, h], me).wait_recv()
            tot = tot + zr[d, h]
        span = pl.ds(h * part, part)
        sums = DECAY_RATE * code_sums[span, :] + (1.0 - DECAY_RATE) * tot[:part]
        counts = DECAY_RATE * code_counts[:, span] + (1.0 - DECAY_RATE) * tot[part : part + 1, :part]
        new_sums[span, :] = sums
        new_counts[:, span] = counts
        new_codebook[span, :] = sums / jnp.transpose(jnp.broadcast_to(counts, (width, part)))
    for cp in pending:
        cp.wait_send()


def local(n, video, clip_start, gain_space, qkv_space, out_space, gain_time, qkv_time, out_time, code_sums, code_counts):
    clips, _, places, width = video.shape
    rows = code_sums.shape[0]
    share, n4 = places // n, n // 4
    halves = 2 if rows >= 256 else 1
    high = rows // halves + 8
    tokens = clips * places
    vmem = pl.BlockSpec(memory_space=pltpu.VMEM)
    dma = pltpu.SemaphoreType.DMA
    lat, sums, counts, book = pl.pallas_call(
        functools.partial(body, n),
        out_shape=(
            jax.ShapeDtypeStruct((clips, n, share, width), F32),
            jax.ShapeDtypeStruct((rows, width), F32),
            jax.ShapeDtypeStruct((1, rows), F32),
            jax.ShapeDtypeStruct((rows, width), F32),
        ),
        in_specs=[vmem, pl.BlockSpec(memory_space=pltpu.SMEM)] + [vmem] * 8,
        out_specs=(vmem,) * 4,
        scratch_shapes=[
            pltpu.VMEM((clips, places, width), F32),
            pltpu.VMEM((clips, n, share, width), F32),
            pltpu.VMEM((n, rows, width), F32),
            pltpu.VMEM((n, rows, tokens), F32),
            pltpu.VMEM((2, tokens, width), BF16),
            pltpu.VMEM((2, tokens, width), BF16),
            pltpu.VMEM((n4, halves, 2, high, width), F32),
            pltpu.VMEM((n4, halves, 2, high, width), F32),
            pltpu.VMEM((n4, halves, 2, high, width), F32),
            pltpu.VMEM((n4, halves, high, width), F32),
            pltpu.VMEM((n4, halves, high, width), F32),
            pltpu.VMEM((n4, halves, high, width), F32),
            pltpu.VMEM((n4, halves, high, width), F32),
            dma((clips, n)), dma((clips, n)),
            dma((n4,)), dma((n4,)),
            dma((n4,)), dma((n4,)),
            dma((2 * n4,)), dma((2 * n4,)),
            dma((n4, halves, 2)), dma((n4, halves, 2)),
            dma((n4, halves)), dma((n4, halves)),
            dma((n4, halves)), dma((n4, halves)),
        ],
        compiler_params=pltpu.CompilerParams(
            collective_id=0, has_side_effects=True, vmem_limit_bytes=60 * 2**20
        ),
        name="tokenizer",
    )(
        video.reshape(clips, places, width), clip_start, gain_space.reshape(1, -1), qkv_space, out_space,
        gain_time.reshape(1, -1), qkv_time, out_time, code_sums, code_counts.reshape(1, -1),
    )
    return lat, sums, counts.reshape(rows), book


def solution(mesh):
    in_specs = (
        P("groups", "frames", None, None),
        P("groups"),
        P(),
        P(),
        P(),
        P(),
        P(),
        P(),
        P(("groups", "frames"), None),
        P(("groups", "frames")),
    )
    out_specs = (
        P("groups", None, "frames", None),
        P(("groups", "frames"), None),
        P(("groups", "frames")),
        P(("groups", "frames"), None),
    )
    fn = functools.partial(local, mesh.shape["frames"])
    return jax.shard_map(fn, mesh=mesh, in_specs=in_specs, out_specs=out_specs, check_vma=False)
```

```python
import functools

import jax
import jax.numpy as jnp
from jax import lax
from jax.experimental import pallas as pl
from jax.experimental.pallas import tpu as pltpu
from jax.sharding import PartitionSpec as P

HEADS = 4
ATTN_SCALE = 10.0
SOFTMAX_WARMTH = 0.05
DECAY_RATE = 0.9
EPSILON = 1e-06
F32 = jnp.float32
BF16 = jnp.bfloat16
NN = (((1,), (0,)), ((), ()))
NT = (((1,), (1,)), ((), ()))


def split(a):
    hi = a.astype(BF16)
    return hi, (a - hi.astype(F32)).astype(BF16)


def dot(a, b, dims=NN):
    return lax.dot_general(a, b, dims, preferred_element_type=F32)


def dot3(a, b, dims=NN):
    return dot(a[0], b[0], dims) + (dot(a[0], b[1], dims) + dot(a[1], b[0], dims))


def dot2(a, b, dims=NN):
    return dot(a[0], b, dims) + dot(a[1], b, dims)


def attention(x, gain, w_qkv, w_out, mask):
    rows, width = x.shape
    hd = width // HEADS
    lane_i = lax.broadcasted_iota(jnp.int32, (width, width), 0) // hd
    lane_j = lax.broadcasted_iota(jnp.int32, (width, width), 1) // hd
    same_head = jnp.where(lane_i == lane_j, 1.0, 0.0).astype(BF16)
    row_head = lax.broadcasted_iota(jnp.int32, (rows, width), 1) // hd

    normed = x * lax.rsqrt(jnp.mean(x * x, -1, keepdims=True) + EPSILON) * gain
    packed = dot3(split(normed), w_qkv)
    q, k, v = packed[:, :width], packed[:, width : 2 * width], packed[:, 2 * width :]
    q = q * lax.rsqrt(dot2(split(q * q), same_head) + EPSILON) * ATTN_SCALE
    k = k * lax.rsqrt(dot2(split(k * k), same_head) + EPSILON)
    qh, ql = split(q)
    ks = split(k)
    vh, vl = split(v)
    mixed = None
    for h in range(HEADS):
        mine = jnp.where(row_head == h, 1.0, 0.0).astype(BF16)
        e = jnp.exp(dot3((qh * mine, ql * mine), ks, NT))
        if mask is not None:
            e = e * mask
        es = split(e)
        o = dot3(es, (vh * mine, vl * mine))
        t = dot2(es, mine)
        mixed, totals = (o, t) if h == 0 else (mixed + o, totals + t)
    return x + dot3(split(mixed / totals), w_out)


def body(
    n,
    video,
    starts,
    gain_space,
    qkv_space,
    out_space,
    gain_time,
    qkv_time,
    out_time,
    code_sums,
    code_counts,
    latents,
    terms,
    acc,
    spaced,
    xin,
    codes,
    weights,
    u_hi,
    u_lo,
    cs,
    ck,
    cr,
    ys,
    yr,
    zs,
    zr,
    a2a_send,
    a2a_recv,
    gz_send,
    gz_recv,
    gy_send,
    gy_recv,
    gc_send,
    gc_recv,
    rc_send,
    rc_recv,
    ry_send,
    ry_recv,
    rz_send,
    rz_recv,
):
    clips, places, width = video.shape
    share = places // n
    rows = code_sums.shape[0]
    n4 = n // 4
    halves = ck.shape[1]
    part = rows // halves
    tokens = clips * places

    me = lax.axis_index("frames")
    zz, b1, b0 = me // 4, (me // 2) % 2, me % 2
    y_mate = zz * 4 + (1 - b1) * 2 + b0
    c_mate = zz * 4 + b1 * 2 + (1 - b0)
    pending = []

    def remote(src, dst, ssem, rsem, dev):
        return pltpu.make_async_remote_copy(
            src_ref=src, dst_ref=dst, send_sem=ssem, recv_sem=rsem,
            device_id={"frames": dev}, device_id_type=pl.DeviceIdType.MESH,
        )

    def send(src, dst, ssem, rsem, dev):
        cp = remote(src, dst, ssem, rsem, dev)
        cp.start()
        pending.append(cp)

    barrier = pltpu.get_barrier_semaphore()

    def greet(i, c):
        pl.semaphore_signal(
            barrier, inc=1, device_id={"frames": lax.rem(me + i, n)},
            device_id_type=pl.DeviceIdType.MESH,
        )
        return c

    lax.fori_loop(1, n, greet, 0)

    own = code_sums[...] / jnp.transpose(jnp.broadcast_to(code_counts[...], (width, rows)))
    own = own * lax.rsqrt(jnp.sum(own * own, -1, keepdims=True) + EPSILON)
    codes[me] = own
    pl.semaphore_wait(barrier, n - 1)

    def block(d, y, c):
        return lax.rem(zz + d, n4) * 4 + y * 2 + c

    def reach(side, s):
        at = zz - s if side == 0 else zz + s
        return at, (at >= 0 if side == 0 else at < n4)

    def slot(side, s):
        return 0 if s == 0 else side * (n4 - 1) + s

    def each(s, do):
        if s == 0:
            do(0, 0)
        else:
            for side in range(2):
                pl.when(reach(side, s)[1])(functools.partial(do, side, s))

    def copy_of(g, ssem, rsem, k, dev):
        return remote(codes.at[g], codes.at[g], ssem.at[k], rsem.at[k], dev)

    def own_block(side, s):
        return reach(side, s)[0] * 4 + b1 * 2 + b0

    def y_block(side, s):
        return reach(side, s)[0] * 4 + (1 - b1) * 2 + b0

    def along(side, s):
        ahead, there = reach(1 - side, 1)
        k = side * n4 + s + 1
        return copy_of(own_block(side, s), gz_send, gz_recv, k, ahead * 4 + b1 * 2 + b0), there

    def forward_own(s):
        def do(side, s):
            g = own_block(side, s)
            if s:
                copy_of(g, gz_send, gz_recv, side * n4 + s, me).wait_recv()
            for sd in range(2) if s == 0 else (side,):
                if s + 1 < n4:
                    cp, there = along(sd, s)
                    pl.when(there)(cp.start)
            k = slot(side, s)
            copy_of(g, gy_send, gy_recv, k, y_mate).start()
            copy_of(g, gc_send, gc_recv, k, c_mate).start()

        each(s, do)

    def forward_y(s):
        def do(side, s):
            g, k = y_block(side, s), slot(side, s)
            copy_of(g, gy_send, gy_recv, k, me).wait_recv()
            copy_of(g, gc_send, gc_recv, 2 * n4 + k, c_mate).start()

        each(s, do)

    def gather_sent(s):
        def do(side, s):
            for sd in range(2) if s == 0 else (side,):
                if s + 1 < n4:
                    cp, there = along(sd, s)
                    pl.when(there)(cp.wait_send)
            g, k = own_block(side, s), slot(side, s)
            copy_of(g, gy_send, gy_recv, k, y_mate).wait_send()
            copy_of(g, gc_send, gc_recv, k, c_mate).wait_send()
            g = y_block(side, s)
            copy_of(g, gc_send, gc_recv, 2 * n4 + k, c_mate).wait_send()

        each(s, do)

    forward_own(0)

    w_q, w_o = split(qkv_space[...]), split(out_space[...])
    gain = gain_space[...]
    for c in range(clips):
        spaced[c] = attention(video[c], gain, w_q, w_o, None)
        for d in range(1, n):
            to = lax.rem(me + d, n)
            send(
                spaced.at[c, pl.ds(pl.multiple_of(to * share, 8), share), :],
                xin.at[c, me], a2a_send.at[c, d], a2a_recv.at[c, d], to,
            )
        xin[c, me] = spaced[c, pl.ds(pl.multiple_of(me * share, 8), share), :]
    if n4 > 1:
        forward_own(1)

    w_q, w_o = split(qkv_time[...]), split(out_time[...])
    gain = gain_time[...]
    bits = share.bit_length() - 1
    r_i = lax.broadcasted_iota(jnp.int32, (places, places), 0)
    r_j = lax.broadcasted_iota(jnp.int32, (places, places), 1)
    t_i, t_j = r_i >> bits, r_j >> bits
    same_place = (r_i & (share - 1)) == (r_j & (share - 1))
    for c in range(clips):
        if c == 1:
            forward_y(0)
        for d in range(1, n):
            src = lax.rem(me + n - d, n)
            remote(xin.at[c, src], xin.at[c, src], a2a_send.at[c, d], a2a_recv.at[c, d], me).wait_recv()
        allowed = same_place & (t_j <= t_i) & ((t_j >= starts[c]) | (t_j == t_i))
        mask = jnp.where(allowed, 1.0, 0.0)
        y = attention(xin[c].reshape(places, width), gain, w_q, w_o, mask)
        latents[c] = y.reshape(n, share, width)
        u = y * lax.rsqrt(jnp.sum(y * y, -1, keepdims=True) + EPSILON)
        u_hi[0, pl.ds(c * places, places), :], u_lo[0, pl.ds(c * places, places), :] = split(u)
        u = u * (1.0 / SOFTMAX_WARMTH)
        u_hi[1, pl.ds(c * places, places), :], u_lo[1, pl.ds(c * places, places), :] = split(u)
    if clips == 1:
        forward_y(0)

    def score(g):
        e = jnp.exp(dot3(split(codes[g]), (u_hi[1], u_lo[1]), NT))
        weights[g] = e
        acc[...] += jnp.sum(e.reshape(rows // 8, 8, tokens), 0)

    def score_all(s):
        def do(side, s):
            at, k = reach(side, s)[0], slot(side, s)
            for y, k in ((b1, k), (1 - b1, 2 * n4 + k)):
                copy_of(at * 4 + y * 2 + (1 - b0), gc_send, gc_recv, k, me).wait_recv()

            def one(i, carry):
                score(at * 4 + i)
                return carry

            lax.fori_loop(0, 4, one, 0)

        each(s, do)

    acc[...] = jnp.zeros((8, tokens), F32)
    for s in range(2, n4 + 2):
        if s < n4:
            forward_own(s)
        if s - 1 < n4:
            forward_y(s - 1)
        score_all(s - 2)
    inv = 1.0 / jnp.sum(acc[...], 0, keepdims=True)
    ones = jnp.ones((8, tokens), BF16)

    def term(g, h, dst):
        ps = split(weights[g, pl.ds(h * part, part), :] * inv)
        dst[pl.ds(0, part), :] = dot3(ps, (u_hi[0], u_lo[0]))
        cnt = dot(ones, ps[0], NT) + dot(ones, ps[1], NT)
        if part < width:
            cnt = jnp.concatenate([cnt, jnp.zeros((8, width - part), F32)], 1)
        dst[pl.ds(part, 8), :] = cnt

    def start(d, h):
        for j in range(2):
            y = lax.rem(b1 + 1 + j, 2)
            term(block(d, y, 1 - b0), h, cs.at[d, h, j])
            send(cs.at[d, h, j], cr.at[d, h, j], rc_send.at[d, h, j], rc_recv.at[d, h, j], c_mate)
        for j in range(2):
            y = lax.rem(b1 + 1 + j, 2)
            term(block(d, y, b0), h, ck.at[d, h, j])

    def wait_core(d, h, j):
        remote(cr.at[d, h, j], cr.at[d, h, j], rc_send.at[d, h, j], rc_recv.at[d, h, j], me).wait_recv()

    def pair(d, h):
        wait_core(d, h, 0)
        ys[d, h] = ck[d, h, 0] + cr[d, h, 0]
        send(ys.at[d, h], yr.at[d, h], ry_send.at[d, h], ry_recv.at[d, h], y_mate)

    def across(d, h):
        wait_core(d, h, 1)
        remote(yr.at[d, h], yr.at[d, h], ry_send.at[d, h], ry_recv.at[d, h], me).wait_recv()
        zs[d, h] = ck[d, h, 1] + cr[d, h, 1] + yr[d, h]
        if d:
            send(zs.at[d, h], zr.at[d, h], rz_send.at[d, h], rz_recv.at[d, h], block(d, b1, b0))

    steps = [(d % n4, h) for d in range(1, n4 + 1) for h in range(halves)]
    total = len(steps)
    for i in range(total + 2):
        if i < total:
            start(*steps[i])
        if 1 <= i <= total:
            pair(*steps[i - 1])
        if i >= 2:
            across(*steps[i - 2])

    for h in range(halves):
        tot = zs[0, h]
        for d in range(1, n4):
            remote(zr.at[d, h], zr.at[d, h], rz_send.at[d, h], rz_recv.at[d, h], me).wait_recv()
            tot = tot + zr[d, h]
        terms[h] = tot
    for s in range(n4):
        gather_sent(s)
    for cp in pending:
        cp.wait_send()


def finish(found, terms, code_sums, code_counts, latents, new_sums, new_counts, new_codebook):
    halves, high, width = terms.shape
    part = high - 8
    latents[...] = found[...]
    for h in range(halves):
        tot = terms[h]
        span = pl.ds(h * part, part)
        sums = DECAY_RATE * code_sums[span, :] + (1.0 - DECAY_RATE) * tot[:part]
        counts = DECAY_RATE * code_counts[:, span] + (1.0 - DECAY_RATE) * tot[part : part + 1, :part]
        new_sums[span, :] = sums
        new_counts[:, span] = counts
        new_codebook[span, :] = sums / jnp.transpose(jnp.broadcast_to(counts, (width, part)))


def local(n, video, clip_start, gain_space, qkv_space, out_space, gain_time, qkv_time, out_time, code_sums, code_counts):
    clips, _, places, width = video.shape
    rows = code_sums.shape[0]
    share, n4 = places // n, n // 4
    halves = 2 if rows >= 256 else 1
    high = rows // halves + 8
    tokens = clips * places
    vmem = pl.BlockSpec(memory_space=pltpu.VMEM)
    dma = pltpu.SemaphoreType.DMA
    found, terms = pl.pallas_call(
        functools.partial(body, n),
        out_shape=(
            jax.ShapeDtypeStruct((clips, n, share, width), F32),
            jax.ShapeDtypeStruct((halves, high, width), F32),
        ),
        in_specs=[vmem, pl.BlockSpec(memory_space=pltpu.SMEM)] + [vmem] * 8,
        out_specs=(vmem,) * 2,
        scratch_shapes=[
            pltpu.VMEM((8, tokens), F32),
            pltpu.VMEM((clips, places, width), F32),
            pltpu.VMEM((clips, n, share, width), F32),
            pltpu.VMEM((n, rows, width), F32),
            pltpu.VMEM((n, rows, tokens), F32),
            pltpu.VMEM((2, tokens, width), BF16),
            pltpu.VMEM((2, tokens, width), BF16),
            pltpu.VMEM((n4, halves, 2, high, width), F32),
            pltpu.VMEM((n4, halves, 2, high, width), F32),
            pltpu.VMEM((n4, halves, 2, high, width), F32),
            pltpu.VMEM((n4, halves, high, width), F32),
            pltpu.VMEM((n4, halves, high, width), F32),
            pltpu.VMEM((n4, halves, high, width), F32),
            pltpu.VMEM((n4, halves, high, width), F32),
            dma((clips, n)), dma((clips, n)),
            dma((2 * n4,)), dma((2 * n4,)),
            dma((2 * n4,)), dma((2 * n4,)),
            dma((4 * n4,)), dma((4 * n4,)),
            dma((n4, halves, 2)), dma((n4, halves, 2)),
            dma((n4, halves)), dma((n4, halves)),
            dma((n4, halves)), dma((n4, halves)),
        ],
        compiler_params=pltpu.CompilerParams(
            collective_id=0, has_side_effects=True, vmem_limit_bytes=60 * 2**20
        ),
        name="tokenizer",
    )(
        video.reshape(clips, places, width), clip_start, gain_space.reshape(1, -1), qkv_space, out_space,
        gain_time.reshape(1, -1), qkv_time, out_time, code_sums, code_counts.reshape(1, -1),
    )
    lat, sums, counts, book = pl.pallas_call(
        finish,
        out_shape=(
            jax.ShapeDtypeStruct((clips, n, share, width), F32),
            jax.ShapeDtypeStruct((rows, width), F32),
            jax.ShapeDtypeStruct((1, rows), F32),
            jax.ShapeDtypeStruct((rows, width), F32),
        ),
        in_specs=[vmem] * 4,
        out_specs=(vmem,) * 4,
        name="finish",
    )(found, terms, code_sums, code_counts.reshape(1, -1))
    return lat, sums, counts.reshape(rows), book


def solution(mesh):
    in_specs = (
        P("groups", "frames", None, None),
        P("groups"),
        P(),
        P(),
        P(),
        P(),
        P(),
        P(),
        P(("groups", "frames"), None),
        P(("groups", "frames")),
    )
    out_specs = (
        P("groups", None, "frames", None),
        P(("groups", "frames"), None),
        P(("groups", "frames")),
        P(("groups", "frames"), None),
    )
    fn = functools.partial(local, mesh.shape["frames"])
    return jax.shard_map(fn, mesh=mesh, in_specs=in_specs, out_specs=out_specs, check_vma=False)
```

```python
import functools

import jax
import jax.numpy as jnp
from jax import lax
from jax.experimental import pallas as pl
from jax.experimental.pallas import tpu as pltpu
from jax.sharding import PartitionSpec as P

HEADS = 4
ATTN_SCALE = 10.0
SOFTMAX_WARMTH = 0.05
DECAY_RATE = 0.9
EPSILON = 1e-06
F32 = jnp.float32
BF16 = jnp.bfloat16
NN = (((1,), (0,)), ((), ()))
NT = (((1,), (1,)), ((), ()))


def split(a):
    hi = a.astype(BF16)
    return hi, (a - hi.astype(F32)).astype(BF16)


def dot(a, b, dims=NN):
    return lax.dot_general(a, b, dims, preferred_element_type=F32)


def dot3(a, b, dims=NN):
    return dot(a[0], b[0], dims) + (dot(a[0], b[1], dims) + dot(a[1], b[0], dims))


def dot2(a, b, dims=NN):
    return dot(a[0], b, dims) + dot(a[1], b, dims)


def attention(x, gain, w_qkv, w_out, mask):
    rows, width = x.shape
    hd = width // HEADS
    lane_i = lax.broadcasted_iota(jnp.int32, (width, width), 0) // hd
    lane_j = lax.broadcasted_iota(jnp.int32, (width, width), 1) // hd
    same_head = jnp.where(lane_i == lane_j, 1.0, 0.0).astype(BF16)
    row_head = lax.broadcasted_iota(jnp.int32, (rows, width), 1) // hd

    normed = x * lax.rsqrt(jnp.mean(x * x, -1, keepdims=True) + EPSILON) * gain
    packed = dot3(split(normed), w_qkv)
    q, k, v = packed[:, :width], packed[:, width : 2 * width], packed[:, 2 * width :]
    q = q * lax.rsqrt(dot2(split(q * q), same_head) + EPSILON) * ATTN_SCALE
    k = k * lax.rsqrt(dot2(split(k * k), same_head) + EPSILON)
    qh, ql = split(q)
    ks = split(k)
    vh, vl = split(v)
    mixed = None
    for h in range(HEADS):
        mine = jnp.where(row_head == h, 1.0, 0.0).astype(BF16)
        e = jnp.exp(dot3((qh * mine, ql * mine), ks, NT))
        if mask is not None:
            e = e * mask
        es = split(e)
        o = dot3(es, (vh * mine, vl * mine))
        t = dot2(es, mine)
        mixed, totals = (o, t) if h == 0 else (mixed + o, totals + t)
    return x + dot3(split(mixed / totals), w_out)


def body(
    n,
    video,
    starts,
    gain_space,
    qkv_space,
    out_space,
    gain_time,
    qkv_time,
    out_time,
    code_sums,
    code_counts,
    latents,
    terms,
    acc,
    spaced,
    xin,
    codes,
    weights,
    u_hi,
    u_lo,
    cs,
    ck,
    cr,
    ys,
    yr,
    zs,
    zr,
    a2a_send,
    a2a_recv,
    gz_send,
    gz_recv,
    gy_send,
    gy_recv,
    gc_send,
    gc_recv,
    rc_send,
    rc_recv,
    ry_send,
    ry_recv,
    rz_send,
    rz_recv,
):
    clips, places, width = video.shape
    share = places // n
    rows = code_sums.shape[0]
    n4 = n // 4
    halves = ck.shape[1]
    part = rows // halves
    tokens = clips * places

    me = lax.axis_index("frames")
    zz, b1, b0 = me // 4, (me // 2) % 2, me % 2
    y_mate = zz * 4 + (1 - b1) * 2 + b0
    c_mate = zz * 4 + b1 * 2 + (1 - b0)
    pending = []

    def remote(src, dst, ssem, rsem, dev):
        return pltpu.make_async_remote_copy(
            src_ref=src, dst_ref=dst, send_sem=ssem, recv_sem=rsem,
            device_id={"frames": dev}, device_id_type=pl.DeviceIdType.MESH,
        )

    def send(src, dst, ssem, rsem, dev):
        cp = remote(src, dst, ssem, rsem, dev)
        cp.start()
        pending.append(cp)

    barrier = pltpu.get_barrier_semaphore()

    def greet(i, c):
        pl.semaphore_signal(
            barrier, inc=1, device_id={"frames": lax.rem(me + i, n)},
            device_id_type=pl.DeviceIdType.MESH,
        )
        return c

    lax.fori_loop(1, n, greet, 0)

    own = code_sums[...] / jnp.transpose(jnp.broadcast_to(code_counts[...], (width, rows)))
    own = own * lax.rsqrt(jnp.sum(own * own, -1, keepdims=True) + EPSILON)
    codes[me] = own
    pl.semaphore_wait(barrier, n - 1)

    def block(d, y, c):
        return lax.rem(zz + d, n4) * 4 + y * 2 + c

    def reach(side, s):
        at = zz - s if side == 0 else zz + s
        return at, (at >= 0 if side == 0 else at < n4)

    def slot(side, s):
        return 0 if s == 0 else side * (n4 - 1) + s

    def each(s, do):
        if s == 0:
            do(0, 0)
        else:
            for side in range(2):
                pl.when(reach(side, s)[1])(functools.partial(do, side, s))

    def copy_of(g, ssem, rsem, k, dev):
        return remote(codes.at[g], codes.at[g], ssem.at[k], rsem.at[k], dev)

    def own_block(side, s):
        return reach(side, s)[0] * 4 + b1 * 2 + b0

    def y_block(side, s):
        return reach(side, s)[0] * 4 + (1 - b1) * 2 + b0

    def along(side, s):
        ahead, there = reach(1 - side, 1)
        k = side * n4 + s + 1
        return copy_of(own_block(side, s), gz_send, gz_recv, k, ahead * 4 + b1 * 2 + b0), there

    def forward_own(s):
        def do(side, s):
            g = own_block(side, s)
            if s:
                copy_of(g, gz_send, gz_recv, side * n4 + s, me).wait_recv()
            for sd in range(2) if s == 0 else (side,):
                if s + 1 < n4:
                    cp, there = along(sd, s)
                    pl.when(there)(cp.start)
            k = slot(side, s)
            copy_of(g, gy_send, gy_recv, k, y_mate).start()
            copy_of(g, gc_send, gc_recv, k, c_mate).start()

        each(s, do)

    def forward_y(s):
        def do(side, s):
            g, k = y_block(side, s), slot(side, s)
            copy_of(g, gy_send, gy_recv, k, me).wait_recv()
            copy_of(g, gc_send, gc_recv, 2 * n4 + k, c_mate).start()

        each(s, do)

    def gather_sent(s):
        def do(side, s):
            for sd in range(2) if s == 0 else (side,):
                if s + 1 < n4:
                    cp, there = along(sd, s)
                    pl.when(there)(cp.wait_send)
            g, k = own_block(side, s), slot(side, s)
            copy_of(g, gy_send, gy_recv, k, y_mate).wait_send()
            copy_of(g, gc_send, gc_recv, k, c_mate).wait_send()
            g = y_block(side, s)
            copy_of(g, gc_send, gc_recv, 2 * n4 + k, c_mate).wait_send()

        each(s, do)

    forward_own(0)

    w_q, w_o = split(qkv_space[...]), split(out_space[...])
    gain = gain_space[...]
    for c in range(clips):
        spaced[c] = attention(video[c], gain, w_q, w_o, None)
        for d in range(1, n):
            to = lax.rem(me + d, n)
            send(
                spaced.at[c, pl.ds(pl.multiple_of(to * share, 8), share), :],
                xin.at[c, me], a2a_send.at[c, d], a2a_recv.at[c, d], to,
            )
        xin[c, me] = spaced[c, pl.ds(pl.multiple_of(me * share, 8), share), :]
    if n4 > 1:
        forward_own(1)

    w_q, w_o = split(qkv_time[...]), split(out_time[...])
    gain = gain_time[...]
    bits = share.bit_length() - 1
    r_i = lax.broadcasted_iota(jnp.int32, (places, places), 0)
    r_j = lax.broadcasted_iota(jnp.int32, (places, places), 1)
    t_i, t_j = r_i >> bits, r_j >> bits
    same_place = (r_i & (share - 1)) == (r_j & (share - 1))
    for c in range(clips):
        if c == 1:
            forward_y(0)
        for d in range(1, n):
            src = lax.rem(me + n - d, n)
            remote(xin.at[c, src], xin.at[c, src], a2a_send.at[c, d], a2a_recv.at[c, d], me).wait_recv()
        allowed = same_place & (t_j <= t_i) & ((t_j >= starts[c]) | (t_j == t_i))
        mask = jnp.where(allowed, 1.0, 0.0)
        y = attention(xin[c].reshape(places, width), gain, w_q, w_o, mask)
        latents[c] = y.reshape(n, share, width)
        u = y * lax.rsqrt(jnp.sum(y * y, -1, keepdims=True) + EPSILON)
        u_hi[0, pl.ds(c * places, places), :], u_lo[0, pl.ds(c * places, places), :] = split(u)
        u = u * (1.0 / SOFTMAX_WARMTH)
        u_hi[1, pl.ds(c * places, places), :], u_lo[1, pl.ds(c * places, places), :] = split(u)
    if clips == 1:
        forward_y(0)

    def score(g):
        e = jnp.exp(dot3(split(codes[g]), (u_hi[1], u_lo[1]), NT))
        weights[g] = e
        acc[...] += jnp.sum(e.reshape(rows // 8, 8, tokens), 0)

    def score_all(s):
        def do(side, s):
            at, k = reach(side, s)[0], slot(side, s)
            for y, k in ((b1, k), (1 - b1, 2 * n4 + k)):
                copy_of(at * 4 + y * 2 + (1 - b0), gc_send, gc_recv, k, me).wait_recv()

            def one(i, carry):
                score(at * 4 + i)
                return carry

            lax.fori_loop(0, 4, one, 0)

        each(s, do)

    acc[...] = jnp.zeros((8, tokens), F32)
    for s in range(2, n4 + 2):
        if s < n4:
            forward_own(s)
        if s - 1 < n4:
            forward_y(s - 1)
        score_all(s - 2)
    inv = 1.0 / jnp.sum(acc[...], 0, keepdims=True)
    ones = jnp.ones((8, tokens), BF16)

    def term(g, h, dst):
        ps = split(weights[g, pl.ds(h * part, part), :] * inv)
        dst[pl.ds(0, part), :] = dot3(ps, (u_hi[0], u_lo[0]))
        cnt = dot(ones, ps[0], NT) + dot(ones, ps[1], NT)
        if part < width:
            cnt = jnp.concatenate([cnt, jnp.zeros((8, width - part), F32)], 1)
        dst[pl.ds(part, 8), :] = cnt

    def start(d, h):
        for j in range(2):
            y = lax.rem(b1 + 1 + j, 2)
            term(block(d, y, 1 - b0), h, cs.at[d, h, j])
            send(cs.at[d, h, j], cr.at[d, h, j], rc_send.at[d, h, j], rc_recv.at[d, h, j], c_mate)
        for j in range(2):
            y = lax.rem(b1 + 1 + j, 2)
            term(block(d, y, b0), h, ck.at[d, h, j])

    def wait_core(d, h, j):
        remote(cr.at[d, h, j], cr.at[d, h, j], rc_send.at[d, h, j], rc_recv.at[d, h, j], me).wait_recv()

    def pair(d, h):
        wait_core(d, h, 0)
        ys[d, h] = ck[d, h, 0] + cr[d, h, 0]
        send(ys.at[d, h], yr.at[d, h], ry_send.at[d, h], ry_recv.at[d, h], y_mate)

    def across(d, h):
        wait_core(d, h, 1)
        remote(yr.at[d, h], yr.at[d, h], ry_send.at[d, h], ry_recv.at[d, h], me).wait_recv()
        zs[d, h] = ck[d, h, 1] + cr[d, h, 1] + yr[d, h]
        if d:
            send(zs.at[d, h], zr.at[d, h], rz_send.at[d, h], rz_recv.at[d, h], block(d, b1, b0))

    steps = [(d % n4, h) for d in range(1, n4 + 1) for h in range(halves)]
    total = len(steps)
    for i in range(total + 2):
        if i < total:
            start(*steps[i])
            pair(*steps[i])
        if i >= 2:
            across(*steps[i - 2])

    for h in range(halves):
        tot = zs[0, h]
        for d in range(1, n4):
            remote(zr.at[d, h], zr.at[d, h], rz_send.at[d, h], rz_recv.at[d, h], me).wait_recv()
            tot = tot + zr[d, h]
        terms[h] = tot
    for s in range(n4):
        gather_sent(s)
    for cp in pending:
        cp.wait_send()


def finish(found, terms, code_sums, code_counts, latents, new_sums, new_counts, new_codebook):
    halves, high, width = terms.shape
    part = high - 8
    latents[...] = found[...]
    for h in range(halves):
        tot = terms[h]
        span = pl.ds(h * part, part)
        sums = DECAY_RATE * code_sums[span, :] + (1.0 - DECAY_RATE) * tot[:part]
        counts = DECAY_RATE * code_counts[:, span] + (1.0 - DECAY_RATE) * tot[part : part + 1, :part]
        new_sums[span, :] = sums
        new_counts[:, span] = counts
        new_codebook[span, :] = sums / jnp.transpose(jnp.broadcast_to(counts, (width, part)))


def local(n, video, clip_start, gain_space, qkv_space, out_space, gain_time, qkv_time, out_time, code_sums, code_counts):
    clips, _, places, width = video.shape
    rows = code_sums.shape[0]
    share, n4 = places // n, n // 4
    halves = 2 if rows >= 256 else 1
    high = rows // halves + 8
    tokens = clips * places
    vmem = pl.BlockSpec(memory_space=pltpu.VMEM)
    dma = pltpu.SemaphoreType.DMA
    found, terms = pl.pallas_call(
        functools.partial(body, n),
        out_shape=(
            jax.ShapeDtypeStruct((clips, n, share, width), F32),
            jax.ShapeDtypeStruct((halves, high, width), F32),
        ),
        in_specs=[vmem, pl.BlockSpec(memory_space=pltpu.SMEM)] + [vmem] * 8,
        out_specs=(vmem,) * 2,
        scratch_shapes=[
            pltpu.VMEM((8, tokens), F32),
            pltpu.VMEM((clips, places, width), F32),
            pltpu.VMEM((clips, n, share, width), F32),
            pltpu.VMEM((n, rows, width), F32),
            pltpu.VMEM((n, rows, tokens), F32),
            pltpu.VMEM((2, tokens, width), BF16),
            pltpu.VMEM((2, tokens, width), BF16),
            pltpu.VMEM((n4, halves, 2, high, width), F32),
            pltpu.VMEM((n4, halves, 2, high, width), F32),
            pltpu.VMEM((n4, halves, 2, high, width), F32),
            pltpu.VMEM((n4, halves, high, width), F32),
            pltpu.VMEM((n4, halves, high, width), F32),
            pltpu.VMEM((n4, halves, high, width), F32),
            pltpu.VMEM((n4, halves, high, width), F32),
            dma((clips, n)), dma((clips, n)),
            dma((2 * n4,)), dma((2 * n4,)),
            dma((2 * n4,)), dma((2 * n4,)),
            dma((4 * n4,)), dma((4 * n4,)),
            dma((n4, halves, 2)), dma((n4, halves, 2)),
            dma((n4, halves)), dma((n4, halves)),
            dma((n4, halves)), dma((n4, halves)),
        ],
        compiler_params=pltpu.CompilerParams(
            collective_id=0, has_side_effects=True, vmem_limit_bytes=60 * 2**20
        ),
        name="tokenizer",
    )(
        video.reshape(clips, places, width), clip_start, gain_space.reshape(1, -1), qkv_space, out_space,
        gain_time.reshape(1, -1), qkv_time, out_time, code_sums, code_counts.reshape(1, -1),
    )
    lat, sums, counts, book = pl.pallas_call(
        finish,
        out_shape=(
            jax.ShapeDtypeStruct((clips, n, share, width), F32),
            jax.ShapeDtypeStruct((rows, width), F32),
            jax.ShapeDtypeStruct((1, rows), F32),
            jax.ShapeDtypeStruct((rows, width), F32),
        ),
        in_specs=[vmem] * 4,
        out_specs=(vmem,) * 4,
        name="finish",
    )(found, terms, code_sums, code_counts.reshape(1, -1))
    return lat, sums, counts.reshape(rows), book


def solution(mesh):
    in_specs = (
        P("groups", "frames", None, None),
        P("groups"),
        P(),
        P(),
        P(),
        P(),
        P(),
        P(),
        P(("groups", "frames"), None),
        P(("groups", "frames")),
    )
    out_specs = (
        P("groups", None, "frames", None),
        P(("groups", "frames"), None),
        P(("groups", "frames")),
        P(("groups", "frames"), None),
    )
    fn = functools.partial(local, mesh.shape["frames"])
    return jax.shard_map(fn, mesh=mesh, in_specs=in_specs, out_specs=out_specs, check_vma=False)
```
